32 devices in a mesh: pole: 2 (over x), row: 8 (over z, y), col: 2 (over core).
Axes of the slice: x: 2, y: 2, z: 4, core: 2. Of those that a mesh axis runs over, the one named last changes fastest.
Arguments:
- inverse_pairs: bfloat16 [4, 12288, 12288], P('pole', 'row', 'col'), parts along dimension 0, may hold values from -0.09375 to 0.09375
- factor_rows: bfloat16 [4, 2, 2048, 256], P('pole', None, 'row', 'col'), parts along dimension 0, may hold values from -1.1953125 to 1.1953125
- diag_blocks: bfloat16 [4, 2, 256, 256], P('pole', None, None, 'col'), parts along dimension 0, may hold values from -6 to 6
- row_lists: int32 [2, 16], replicated, may hold values from 0 to 95, as said below
- block_order: int32 [96], replicated, may hold values from 0 to 95, each once
Outputs:
- inv_cols: float32 [4, 2, 12288, 256], P('pole', None, 'row', 'col'), parts along dimension 0
- schur_blocks: float32 [4, 2, 256, 256], P('pole', None, None, 'col'), parts along dimension 0
The draws below stay inside these ranges and needn't reach their ends.
There are 2 independent parts, one for each index of `pole`. The reference program is written for one: setup_inputs(seed, part) draws one part's arguments, and reference() takes and returns one part's arrays. A program takes and returns all parts, laid end to end along the dimension named above; an argument that names none is the same for every part. Nothing has to cross between parts.
Inputs may be any that keep to these rules, and one draw needn't show every extreme that they name: `row_lists`: each of the 2 rows holds 16 different block numbers in increasing order, always including 0 and 95.
All inputs are finite; a program needn't handle non-finite values.
Results may differ from the reference program's by a relative error of at most 0.0003.
Values may be sent and summed in bfloat16 or wider, within the bound.
A program may use at most 128 MiB of HBM per device.

```python
import jax
import jax.numpy as jnp
from jax import lax

NSN = 2
W = 256
MA = 12288
BLK = 128
R = 16
NB = 96
LROWS = 2048


def draw_row_lists(key, part):
    lists = []
    for supernode in range(NSN):
        inner = jax.random.permutation(jax.random.fold_in(key, 101 + supernode), NB - 2).astype(jnp.int32) + 1
        chosen = jnp.concatenate([jnp.zeros((1,), jnp.int32), inner[:R - 2], jnp.full((1,), NB - 1, jnp.int32)])
        lists.append(jnp.sort(chosen))
    return jnp.stack(lists).astype(jnp.int32)


def block_levels(rng, dims, cuts, least, high):
    factor_of = 1.0
    for axis_at, shards_of in cuts:
        steps = jax.random.uniform(jax.random.fold_in(jax.random.fold_in(rng, 6), axis_at), (shards_of,), jnp.float32, least / len(cuts), high / len(cuts))
        factor_of = factor_of * jnp.repeat(jnp.exp(steps), dims[axis_at] // shards_of).reshape((-1,) + (1,) * (len(dims) - 1 - axis_at))
    return factor_of


def normal_values(key, shape, deviation, bound, shards=(), held_as=jnp.bfloat16):
    result = deviation * jax.random.normal(key, shape, jnp.float32)
    if shards:
        result = result * block_levels(key, shape, shards, -0.22, 0.18)
    return jnp.clip(result, -bound, bound).astype(held_as)


def setup_inputs(seed: int = 0, part: int = 0) -> dict:
    splits = jax.random.split(jax.random.key(seed), 6)
    part_keys = jax.random.split(jax.random.fold_in(splits[5], part), 6)
    return {
        "inverse_pairs": normal_values(part_keys[0], (2, MA, MA), (2 * LROWS) ** -0.5, 0.09375, ((1, 8), (2, 2))),
        "factor_rows": normal_values(part_keys[1], (NSN, 2, LROWS, W), 0.2, 1.1953125, ((2, 8), (3, 2))),
        "diag_blocks": normal_values(part_keys[2], (NSN, 2, W, W), 1.0, 6.0, ((3, 2),)),
        "row_lists": draw_row_lists(jax.random.fold_in(splits[5], 71), part),
        "block_order": jax.random.permutation(splits[4], NB).astype(jnp.int32),
    }


def reference(inverse_pairs, factor_rows, diag_blocks, row_lists, block_order):
    columns = inverse_pairs.reshape(2, MA, NB, BLK)
    storage = jnp.arange(NB, dtype=jnp.int32)
    cols_list = []
    schur_list = []
    for supernode in range(NSN):
        hits = block_order[None, :] == row_lists[supernode][:, None]
        position = jnp.sum(jnp.where(hits, storage[None, :], 0), axis=1).astype(jnp.int32)
        chosen = jnp.take(columns, position, axis=2).reshape(2, MA, LROWS)
        factor = factor_rows[supernode]
        real_part = jnp.dot(chosen[0], factor[0], preferred_element_type=jnp.float32) - jnp.dot(chosen[1], factor[1], preferred_element_type=jnp.float32)
        imag_part = jnp.dot(chosen[0], factor[1], preferred_element_type=jnp.float32) + jnp.dot(chosen[1], factor[0], preferred_element_type=jnp.float32)
        values = -jnp.stack([real_part, imag_part])
        listed = jnp.take(values.reshape(2, NB, BLK, W), position, axis=1).reshape(2, LROWS, W)
        factor_wide = factor.astype(jnp.float32)
        highest = lax.Precision.HIGHEST
        gram_real = jnp.dot(factor_wide[0].T, listed[0], precision=highest) - jnp.dot(factor_wide[1].T, listed[1], precision=highest)
        gram_imag = jnp.dot(factor_wide[0].T, listed[1], precision=highest) + jnp.dot(factor_wide[1].T, listed[0], precision=highest)
        schur = diag_blocks[supernode].astype(jnp.float32) - jnp.stack([gram_real, gram_imag])
        cols_list.append(values)
        schur_list.append(schur)
    return jnp.stack(cols_list), jnp.stack(schur_list)
```

```python
import functools

import jax
import jax.numpy as jnp
from jax import lax
from jax.experimental import pallas as pl
from jax.experimental.pallas import tpu as pltpu
from jax.sharding import PartitionSpec as P

NSN = 2
BLK = 128
MESH = pl.DeviceIdType.MESH
ANY = pl.BlockSpec(memory_space=pl.ANY)
VMEM = pl.BlockSpec(memory_space=pltpu.VMEM)
SMEM = pl.BlockSpec(memory_space=pltpu.SMEM)


def gather_kernel(n, ny, x_ref, g_ref, loc_sem, zs_send, zs_recv, y_send, y_recv, s_send, s_recv):
    nz = n // ny
    span = x_ref.shape[2]
    row = lax.axis_index("row")
    col = lax.axis_index("col")
    z = row // ny
    y = row % ny
    oy = ny - 1 - y
    sibling = {"col": 1 - col}
    up = {"row": row + ny}
    down = {"row": row - ny}
    across = {"row": z * ny + oy}

    barrier = pltpu.get_barrier_semaphore()
    pl.semaphore_signal(barrier, inc=1, device_id=sibling, device_id_type=MESH)
    pl.semaphore_signal(barrier, inc=1, device_id=across, device_id_type=MESH)

    @pl.when(z < nz - 1)
    def _():
        pl.semaphore_signal(barrier, inc=1, device_id=up, device_id_type=MESH)

    @pl.when(z > 0)
    def _():
        pl.semaphore_signal(barrier, inc=1, device_id=down, device_id_type=MESH)

    pl.semaphore_wait(barrier, 2 + (z < nz - 1).astype(jnp.int32) + (z > 0).astype(jnp.int32))

    def slot(c, r):
        return g_ref.at[c, :, :, pl.ds(pl.multiple_of(r * span, span), span), :]

    def copy(src, c, r, send, recv, target):
        return pltpu.make_async_remote_copy(
            src_ref=src, dst_ref=slot(c, r), send_sem=send, recv_sem=recv,
            device_id=target, device_id_type=MESH,
        )

    def line(src, zz, target):
        return copy(src, col, zz * ny + y, zs_send.at[zz], zs_recv.at[zz], target)

    def side(src, zz, yy):
        return copy(src, col, zz * ny + yy, y_send.at[zz], y_recv.at[zz], across)

    def sib(src, c, r):
        return copy(src, c, r, s_send.at[r], s_recv.at[r], sibling)

    def here(zz, yy):
        return slot(col, zz * ny + yy)

    @pl.when(z < nz - 1)
    def _():
        copy(x_ref, col, row, zs_send.at[nz], zs_recv.at[z], up).start()

    @pl.when(z > 0)
    def _():
        copy(x_ref, col, row, zs_send.at[nz + 1], zs_recv.at[z], down).start()

    side(x_ref, z, y).start()
    sib(x_ref, col, row).start()
    local = pltpu.make_async_copy(x_ref, slot(col, row), loc_sem)
    local.start()

    def from_line(zz, forward, target):
        line(here(zz, y), zz, target).wait_recv()

        @pl.when(forward)
        def _():
            line(here(zz, y), zz, target).start()

        side(here(zz, y), zz, y).start()
        sib(here(zz, y), col, zz * ny + y).start()

    def from_side(zz):
        side(here(zz, oy), zz, oy).wait_recv()
        sib(here(zz, oy), col, zz * ny + oy).start()

    for d in range(1, nz + 1):
        for zz, seen in ((z - d + 1, True), (z + d - 1, d > 1)):
            if seen:
                @pl.when((zz >= 0) & (zz < nz))
                def _():
                    from_side(zz)
        if d < nz:
            @pl.when(z - d >= 0)
            def _():
                from_line(z - d, z < nz - 1, up)

            @pl.when(z + d < nz)
            def _():
                from_line(z + d, z > 0, down)

    local.wait()
    for r in range(n):
        sib(slot(1 - col, r), 1 - col, r).wait_recv()
    for r in range(n):
        sib(slot(col, r), col, r).wait_send()
    for zz in range(nz):
        side(here(zz, y), zz, y).wait_send()

        @pl.when(((zz < z) & (z < nz - 1)) | ((zz > z) & (z > 0)))
        def _():
            line(here(zz, y), zz, up).wait_send()

    @pl.when(z < nz - 1)
    def _():
        copy(x_ref, col, row, zs_send.at[nz], zs_recv.at[z], up).wait_send()

    @pl.when(z > 0)
    def _():
        copy(x_ref, col, row, zs_send.at[nz + 1], zs_recv.at[z], down).wait_send()


def gather(n, x):
    ny = 2 if n % 2 == 0 else 1
    nz = n // ny
    dma = pltpu.SemaphoreType.DMA
    return pl.pallas_call(
        functools.partial(gather_kernel, n, ny),
        out_shape=jax.ShapeDtypeStruct((2, NSN, 2, n * x.shape[2], x.shape[3]), x.dtype),
        in_specs=[ANY],
        out_specs=ANY,
        scratch_shapes=[dma, dma((nz + 2,)), dma((nz,)), dma((nz,)), dma((nz,)), dma((n,)), dma((n,))],
        compiler_params=pltpu.CompilerParams(collective_id=0, has_side_effects=True),
        name="gather_factor",
    )(x)


def product_kernel(listed, blocks_col, blocks_row, meta, g_ref, a_ref, own_ref, oth_ref, gram_ref,
                   abuf, bbuf, entry, sems):
    rows = a_ref.shape[1]
    tile = 256 if rows % 256 == 0 else BLK
    col = meta[2 * NSN, 0]

    def fetch(k, s, block):
        pair = s // 2
        for part in range(2):
            lane = pl.multiple_of((s % 2) * 2 * BLK + part * BLK, BLK)
            pltpu.make_async_copy(
                a_ref.at[part, :, pl.ds(pl.multiple_of(block * BLK, BLK), BLK)],
                abuf.at[k, pair, :, pl.ds(lane, BLK)],
                sems.at[k, pair],
            ).start()

    counts = []
    for k in range(NSN):
        def scan(j, count, k=k):
            block = meta[k, j]
            inside = (block >= 0) & (block < blocks_col)

            @pl.when(inside)
            def _():
                entry[k, count] = j
                fetch(k, count, block)

            return count + inside.astype(jnp.int32)

        count = lax.fori_loop(0, listed, scan, jnp.int32(0))

        @pl.when(count % 2 == 1)
        def _(k=k, count=count):
            fetch(k, count, meta[k, entry[k, count - 1]])

        counts.append(count)

    own_ref[...] = jnp.zeros_like(own_ref)
    oth_ref[...] = jnp.zeros_like(oth_ref)
    gram_ref[...] = jnp.zeros_like(gram_ref)
    outs = (own_ref, oth_ref)
    for k in range(NSN):
        count = counts[k]

        def step(pair, carry, k=k, count=count):
            for half in range(2):
                s = pair * 2 + half
                base = half * 2 * BLK

                @pl.when(s < count)
                def _():
                    at = pl.ds(pl.multiple_of(entry[k, s] * BLK, BLK), BLK)
                    for rel in range(2):
                        c = col if rel == 0 else 1 - col
                        real = g_ref[c, k, 0, at, :]
                        imag = g_ref[c, k, 1, at, :]
                        left = rel * 2 * BLK
                        bbuf[base:base + BLK, left:left + BLK] = -real
                        bbuf[base:base + BLK, left + BLK:left + 2 * BLK] = -imag
                        bbuf[base + BLK:base + 2 * BLK, left:left + BLK] = imag
                        bbuf[base + BLK:base + 2 * BLK, left + BLK:left + 2 * BLK] = -real

                @pl.when(s >= count)
                def _():
                    bbuf[base:base + 2 * BLK, :] = jnp.zeros((2 * BLK, 4 * BLK), jnp.bfloat16)

            pltpu.make_async_copy(abuf.at[k, pair], abuf.at[k, pair], sems.at[k, pair]).wait()

            def by_tile(t, inner):
                at = pl.ds(pl.multiple_of(t * tile, tile), tile)
                left = abuf[k, pair, at, :]
                for rel in range(2):
                    found = jnp.dot(left, bbuf[:, rel * 2 * BLK:(rel + 1) * 2 * BLK],
                                    preferred_element_type=jnp.float32)
                    outs[rel][k, 0, at, :] += found[:, :BLK]
                    outs[rel][k, 1, at, :] += found[:, BLK:]
                return inner

            lax.fori_loop(0, rows // tile, by_tile, 0)
            return carry

        lax.fori_loop(0, (count + 1) // 2, step, 0)

        def correct(j, carry, k=k):
            block = meta[NSN + k, j]

            @pl.when((block >= 0) & (block < blocks_row))
            def _():
                at = pl.ds(pl.multiple_of(j * BLK, BLK), BLK)
                here = pl.ds(pl.multiple_of(block * BLK, BLK), BLK)
                factor = jnp.concatenate([
                    jnp.concatenate([g_ref[0, k, 0, at, :], g_ref[1, k, 0, at, :]], axis=1),
                    jnp.concatenate([g_ref[0, k, 1, at, :], g_ref[1, k, 1, at, :]], axis=1),
                ], axis=0)
                for rel in range(2):
                    real = outs[rel][k, 0, here, :]
                    imag = outs[rel][k, 1, here, :]
                    wide = jnp.concatenate([
                        jnp.concatenate([real, imag], axis=1),
                        jnp.concatenate([-imag, real], axis=1),
                    ], axis=0)
                    total = None
                    for _ in range(3):
                        piece = wide.astype(jnp.bfloat16)
                        wide = wide - piece.astype(jnp.float32)
                        term = lax.dot_general(factor, piece, (((0,), (0,)), ((), ())),
                                               preferred_element_type=jnp.float32)
                        total = term if total is None else total + term
                    gram_ref[rel, k, 0] += total[:, :BLK]
                    gram_ref[rel, k, 1] += total[:, BLK:]

            return carry

        lax.fori_loop(0, listed, correct, 0)


def products(meta, g, a, listed, blocks_col, blocks_row):
    rows = a.shape[1]
    width = 2 * g.shape[4]
    pairs = (listed + 1) // 2
    half = jax.ShapeDtypeStruct((NSN, 2, rows, BLK), jnp.float32)
    return pl.pallas_call(
        functools.partial(product_kernel, listed, blocks_col, blocks_row),
        out_shape=(half, half, jax.ShapeDtypeStruct((2, NSN, 2, width, BLK), jnp.float32)),
        in_specs=[SMEM, VMEM, ANY],
        out_specs=(VMEM, VMEM, VMEM),
        scratch_shapes=[
            pltpu.VMEM((NSN, pairs, rows, 4 * BLK), jnp.bfloat16),
            pltpu.VMEM((4 * BLK, 4 * BLK), jnp.bfloat16),
            pltpu.SMEM((NSN, listed), jnp.int32),
            pltpu.SemaphoreType.DMA((NSN, pairs)),
        ],
        compiler_params=pltpu.CompilerParams(vmem_limit_bytes=56 * 1024 * 1024),
        name="listed_products",
    )(meta, g, a)


def reduce_kernel(n, oth_ref, gram_ref, recv_ref, sum_ref, pair, mine, parts,
                  p_send, p_recv, g_send, g_recv, r_send, r_recv, b_send, b_recv):
    row = lax.axis_index("row")
    col = lax.axis_index("col")
    sibling = {"col": 1 - col}
    size = sum_ref.shape[0] // n

    barrier = pltpu.get_barrier_semaphore()
    pl.semaphore_signal(barrier, inc=1, device_id=sibling, device_id_type=MESH)
    for d in range(1, n):
        pl.semaphore_signal(barrier, inc=1, device_id={"row": (row + d) % n}, device_id_type=MESH)
    pl.semaphore_wait(barrier, n)

    halves = pltpu.make_async_remote_copy(
        src_ref=gram_ref.at[1], dst_ref=pair, send_sem=g_send, recv_sem=g_recv,
        device_id=sibling, device_id_type=MESH)
    halves.start()
    values = pltpu.make_async_remote_copy(
        src_ref=oth_ref, dst_ref=recv_ref, send_sem=p_send, recv_sem=p_recv,
        device_id=sibling, device_id_type=MESH)
    values.start()
    halves.wait()
    mine[...] = gram_ref[0] + pair[...]

    def at(r):
        return pl.ds(pl.multiple_of(r * size, size), size)

    def scatter(d):
        to = (row + d) % n
        return pltpu.make_async_remote_copy(
            src_ref=mine.at[at(to)], dst_ref=parts.at[d], send_sem=r_send.at[d], recv_sem=r_recv.at[d],
            device_id={"row": to}, device_id_type=MESH)

    def spread(d):
        return pltpu.make_async_remote_copy(
            src_ref=parts.at[0], dst_ref=sum_ref.at[at(row)], send_sem=b_send.at[d], recv_sem=b_recv.at[d],
            device_id={"row": (row + d) % n}, device_id_type=MESH)

    for d in range(1, n):
        scatter(d).start()
    total = mine[at(row), :]
    for d in range(1, n):
        scatter(d).wait_recv()
        total = total + parts[d]
    parts[0] = total
    sum_ref[at(row), :] = total
    for d in range(1, n):
        spread(d).start()
    for d in range(1, n):
        scatter(d).wait_send()
    for d in range(1, n):
        spread(d).wait()
    values.wait()


def reduce(n, oth, gram):
    size = gram.shape[1] * gram.shape[2] * gram.shape[3]
    flat = gram.reshape(2, size, BLK)
    dma = pltpu.SemaphoreType.DMA
    return pl.pallas_call(
        functools.partial(reduce_kernel, n),
        out_shape=(jax.ShapeDtypeStruct(oth.shape, oth.dtype), jax.ShapeDtypeStruct((size, BLK), jnp.float32)),
        in_specs=[ANY, VMEM],
        out_specs=(ANY, VMEM),
        scratch_shapes=[
            pltpu.VMEM((size, BLK), jnp.float32),
            pltpu.VMEM((size, BLK), jnp.float32),
            pltpu.VMEM((n, size // n, BLK), jnp.float32),
            dma, dma, dma, dma, dma((n,)), dma((n,)), dma((n,)), dma((n,)),
        ],
        compiler_params=pltpu.CompilerParams(collective_id=1, has_side_effects=True),
        name="reduce_parts",
    )(oth, flat)


def local(n, inverse_pairs, factor_rows, diag_blocks, row_lists, block_order):
    blocks_row = inverse_pairs.shape[1] // BLK
    blocks_col = inverse_pairs.shape[2] // BLK
    listed = row_lists.shape[1]
    col = lax.axis_index("col")
    hits = row_lists[:, :, None] == block_order[None, None, :]
    storage = jnp.arange(block_order.shape[0], dtype=jnp.int32)
    position = jnp.sum(jnp.where(hits, storage, 0), axis=2).astype(jnp.int32)
    meta = jnp.concatenate([
        position - col * blocks_col,
        position - lax.axis_index("row") * blocks_row,
        jnp.full((1, listed), col, jnp.int32),
    ], axis=0)
    g = gather(n, factor_rows)
    own, oth, gram = products(meta, g, inverse_pairs, listed, blocks_col, blocks_row)
    received, correction = reduce(n, oth, gram)
    schur = diag_blocks.astype(jnp.float32) - correction.reshape(diag_blocks.shape)
    return (own + received, schur)


def solution(mesh):
    in_specs = (
        P("pole", "row", "col"),
        P("pole", None, "row", "col"),
        P("pole", None, None, "col"),
        P(),
        P(),
    )
    out_specs = (P("pole", None, "row", "col"), P("pole", None, None, "col"))
    return jax.shard_map(functools.partial(local, mesh.shape["row"]), mesh=mesh, in_specs=in_specs,
                         out_specs=out_specs, check_vma=False)
```

```python
import functools

import jax
import jax.numpy as jnp
from jax import lax
from jax.experimental import pallas as pl
from jax.experimental.pallas import tpu as pltpu
from jax.sharding import PartitionSpec as P

NSN = 2
BLK = 128
MESH = pl.DeviceIdType.MESH
ANY = pl.BlockSpec(memory_space=pl.ANY)
VMEM = pl.BlockSpec(memory_space=pltpu.VMEM)
SMEM = pl.BlockSpec(memory_space=pltpu.SMEM)


def aligned(start, size):
    return pl.ds(pl.multiple_of(start, size), size)


def kernel(n, ny, pick, keep, local_pick, local_keep, x_ref, a_ref, out_ref, sum_ref,
           a_buf, g_ref, own, oth, recv, bbuf, mine, parts,
           a_sem, loc_sem, z_send, z_recv, y_send, y_recv, s_send, s_recv,
           v_send, v_recv, o_sem, r_send, r_recv, b_send, b_recv):
    nz = n // ny
    span = g_ref.shape[3] * BLK // n
    rows = a_ref.shape[1]
    blocks_col = a_ref.shape[2] // BLK
    blocks_row = rows // BLK
    tile = 512 if rows % 512 == 0 else 384 if rows % 384 == 0 else BLK
    per = max(1, span // BLK)
    unit = min(span, BLK)
    row = lax.axis_index("row")
    col = lax.axis_index("col")
    z = row // ny
    y = row % ny
    oy = ny - 1 - y
    sibling = {"col": 1 - col}
    up = {"row": row + ny}
    down = {"row": row - ny}
    across = {"row": z * ny + oy}

    def stream(b):
        return pltpu.make_async_copy(a_ref.at[:, :, aligned(b * BLK, BLK)], a_buf.at[b], a_sem.at[b])

    def start_stream(b, carry):
        stream(b).start()
        return carry

    def wait_stream(b, carry):
        stream(b).wait()
        return carry

    def slot(c, r):
        if span >= BLK:
            return g_ref.at[c, :, :, pl.ds(r * per, per)]
        return g_ref.at[c, :, :, r * span // BLK, aligned(r * span % BLK, span)]

    local = pltpu.make_async_copy(x_ref, slot(col, row), loc_sem)
    local.start()

    barrier = pltpu.get_barrier_semaphore()
    pl.semaphore_signal(barrier, inc=1, device_id=sibling, device_id_type=MESH)
    for d in range(1, n):
        pl.semaphore_signal(barrier, inc=1, device_id={"row": (row + d) % n}, device_id_type=MESH)
    pl.semaphore_wait(barrier, n)

    def copy(src, c, r, send, got, target):
        return pltpu.make_async_remote_copy(
            src_ref=src, dst_ref=slot(c, r), send_sem=send, recv_sem=got,
            device_id=target, device_id_type=MESH)

    def line(src, zz, target):
        return copy(src, col, zz * ny + y, z_send.at[zz], z_recv.at[zz], target)

    def side(src, zz, yy):
        return copy(src, col, zz * ny + yy, y_send.at[zz], y_recv.at[zz], across)

    def sib(src, c, r):
        return copy(src, c, r, s_send.at[r], s_recv.at[r], sibling)

    def here(zz, yy):
        return slot(col, zz * ny + yy)

    first_up = copy(x_ref, col, row, z_send.at[nz], z_recv.at[z], up)
    first_down = copy(x_ref, col, row, z_send.at[nz + 1], z_recv.at[z], down)
    pl.when(z < nz - 1)(lambda: first_up.start())
    pl.when(z > 0)(lambda: first_down.start())
    side(x_ref, z, y).start()
    sib(x_ref, col, row).start()
    lax.fori_loop(0, blocks_col, start_stream, 0)
    own[...] = jnp.zeros_like(own)
    oth[...] = jnp.zeros_like(oth)
    mine[...] = jnp.zeros_like(mine)
    local.wait()

    def from_line(zz, forward, target):
        line(here(zz, y), zz, target).wait_recv()

        @pl.when(forward)
        def _():
            line(here(zz, y), zz, target).start()

        side(here(zz, y), zz, y).start()
        sib(here(zz, y), col, zz * ny + y).start()

    def from_side(zz):
        side(here(zz, oy), zz, oy).wait_recv()
        sib(here(zz, oy), col, zz * ny + oy).start()

    outs = (own, oth)

    def multiply(r):
        sib(slot(1 - col, r), 1 - col, r).wait_recv()

        def supernode(k, carry):
            if unit < BLK:
                bbuf[...] = jnp.zeros_like(bbuf)
            for e in range(per):
                start = r * span + e * BLK
                scale = keep[k, start // BLK]
                base = e * 2 * BLK
                if unit < BLK:
                    shift = start % BLK
                    top = aligned(base + shift, unit)
                    low = aligned(base + BLK + shift, unit)
                else:
                    top = pl.ds(base, unit)
                    low = pl.ds(base + BLK, unit)
                for rel in range(2):
                    c = col if rel == 0 else 1 - col
                    at = pl.ds(0, unit) if unit == BLK else aligned(start % BLK, unit)
                    real = (g_ref[c, k, 0, start // BLK, at, :].astype(jnp.float32) * scale).astype(jnp.bfloat16)
                    imag = (g_ref[c, k, 1, start // BLK, at, :].astype(jnp.float32) * scale).astype(jnp.bfloat16)
                    left = rel * 2 * BLK
                    bbuf[top, left:left + BLK] = -real
                    bbuf[top, left + BLK:left + 2 * BLK] = -imag
                    bbuf[low, left:left + BLK] = imag
                    bbuf[low, left + BLK:left + 2 * BLK] = -real

            def by_tile(t, inner):
                at = aligned(t * tile, tile)
                pieces = []
                for e in range(per):
                    block = pick[k, (r * span + e * BLK) // BLK]
                    pieces += [a_buf[block, 0, at, :], a_buf[block, 1, at, :]]
                left = jnp.concatenate(pieces, axis=1)
                for rel in range(2):
                    found = jnp.dot(left, bbuf[:, rel * 2 * BLK:(rel + 1) * 2 * BLK],
                                    preferred_element_type=jnp.float32)
                    outs[rel][k, 0, at, :] += found[:, :BLK]
                    outs[rel][k, 1, at, :] += found[:, BLK:]
                return inner

            lax.fori_loop(0, rows // tile, by_tile, 0)
            return carry

        lax.fori_loop(0, NSN, supernode, 0)

    def one_round(d, carry):
        pl.when(z - d >= 0)(lambda: from_line(z - d, z < nz - 1, up))
        pl.when(z + d < nz)(lambda: from_line(z + d, z > 0, down))
        pl.when(z - d + 1 >= 0)(lambda: from_side(z - d + 1))
        pl.when((d > 1) & (z + d - 1 < nz))(lambda: from_side(z + d - 1))

        @pl.when(d == 2)
        def _():
            lax.fori_loop(0, blocks_col, wait_stream, 0)


        def late(q, inner):
            away = d - 2 - q // 2
            zz = z + jnp.where(q % 2 == 0, -away, away)
            yy = jnp.where(q // 2 == 0, y, oy)
            valid = (away >= 0) & (zz >= 0) & (zz < nz) & ((away > 0) | (q % 2 == 0))
            pl.when(valid)(lambda: multiply(zz * ny + yy))
            return inner

        lax.fori_loop(0, 4, late, 0)
        return carry

    lax.fori_loop(1, nz + 3, one_round, 0)

    def swap(k):
        return pltpu.make_async_remote_copy(
            src_ref=oth.at[k], dst_ref=recv.at[k], send_sem=v_send.at[k], recv_sem=v_recv.at[k],
            device_id=sibling, device_id_type=MESH)

    for k in range(NSN):
        swap(k).start()
    for r in range(n):
        sib(slot(col, r), col, r).wait_send()
    for zz in range(nz):
        side(here(zz, y), zz, y).wait_send()
        pl.when(((zz < z) & (z < nz - 1)) | ((zz > z) & (z > 0)))(
            lambda: line(here(zz, y), zz, up).wait_send())
    pl.when(z < nz - 1)(lambda: first_up.wait_send())
    pl.when(z > 0)(lambda: first_down.wait_send())

    group = 3 if blocks_row % 3 == 0 else 1
    width = 2 * BLK
    for k in range(NSN):
        swap(k).wait_recv()
        own[k] += recv[k]
        pltpu.make_async_copy(own.at[k], out_ref.at[k], o_sem.at[k]).start()

        def correct(s, carry, k=k):
            left, right = [], []
            for u in range(group):
                t = s * group + u
                j = local_pick[k, t]
                scale = local_keep[k, t]
                for p in range(2):
                    left.append(jnp.concatenate([g_ref[0, k, p, j], g_ref[1, k, p, j]], axis=1))
                real = own[k, 0, aligned(t * BLK, BLK), :] * scale
                imag = own[k, 1, aligned(t * BLK, BLK), :] * scale
                right.append(jnp.concatenate([real, imag], axis=1))
                right.append(jnp.concatenate([-imag, real], axis=1))
            factor = jnp.concatenate(left, axis=0)
            wide = jnp.concatenate(right, axis=0)
            total = None
            for _ in range(3):
                piece = wide.astype(jnp.bfloat16)
                wide = wide - piece.astype(jnp.float32)
                term = lax.dot_general(factor, piece, (((0,), (0,)), ((), ())),
                                       preferred_element_type=jnp.float32)
                total = term if total is None else total + term
            mine[2 * k * width:(2 * k + 1) * width, :] += total[:, :BLK]
            mine[(2 * k + 1) * width:(2 * k + 2) * width, :] += total[:, BLK:]
            return carry

        lax.fori_loop(0, blocks_row // group, correct, 0)

    size = sum_ref.shape[0] // n

    def scatter(d):
        to = (row + d) % n
        return pltpu.make_async_remote_copy(
            src_ref=mine.at[aligned(to * size, size)], dst_ref=parts.at[d],
            send_sem=r_send.at[d], recv_sem=r_recv.at[d],
            device_id={"row": to}, device_id_type=MESH)

    def spread(d):
        return pltpu.make_async_remote_copy(
            src_ref=parts.at[0], dst_ref=sum_ref.at[aligned(row * size, size)],
            send_sem=b_send.at[d], recv_sem=b_recv.at[d],
            device_id={"row": (row + d) % n}, device_id_type=MESH)

    for d in range(1, n):
        scatter(d).start()
    total = mine[aligned(row * size, size), :]
    for d in range(1, n):
        scatter(d).wait_recv()
        total = total + parts[d]
    parts[0] = total
    sum_ref[aligned(row * size, size), :] = total
    for d in range(1, n):
        spread(d).start()
    for k in range(NSN):
        swap(k).wait_send()
        pltpu.make_async_copy(own.at[k], out_ref.at[k], o_sem.at[k]).wait()
    for d in range(1, n):
        scatter(d).wait_send()
    for d in range(1, n):
        spread(d).wait()


def local(n, inverse_pairs, factor_rows, diag_blocks, row_lists, block_order):
    rows, cols = inverse_pairs.shape[1:]
    blocks_row, blocks_col = rows // BLK, cols // BLK
    listed = row_lists.shape[1]
    hits = row_lists[:, :, None] == block_order[None, None, :]
    storage = jnp.arange(block_order.shape[0], dtype=jnp.int32)
    position = jnp.sum(jnp.where(hits, storage, 0), axis=2).astype(jnp.int32)
    pick = position - lax.axis_index("col") * blocks_col
    keep = ((pick >= 0) & (pick < blocks_col)).astype(jnp.float32)
    pick = jnp.clip(pick, 0, blocks_col - 1)
    place = lax.axis_index("row") * blocks_row + jnp.arange(blocks_row, dtype=jnp.int32)
    found = position[:, None, :] == place[None, :, None]
    local_pick = jnp.sum(jnp.where(found, jnp.arange(listed, dtype=jnp.int32), 0), axis=2).astype(jnp.int32)
    local_keep = jnp.sum(found.astype(jnp.float32), axis=2)

    ny = 2 if n % 2 == 0 else 1
    nz = n // ny
    span, half = factor_rows.shape[2:]
    size = NSN * 2 * 2 * half
    per = max(1, span // BLK)
    shards = factor_rows.reshape(NSN, 2, per, BLK, half) if span >= BLK else factor_rows
    dma = pltpu.SemaphoreType.DMA
    side = (NSN, 2, rows, half)
    values, correction = pl.pallas_call(
        functools.partial(kernel, n, ny),
        out_shape=(jax.ShapeDtypeStruct(side, jnp.float32), jax.ShapeDtypeStruct((size, half), jnp.float32)),
        in_specs=[SMEM, SMEM, SMEM, SMEM, ANY, ANY],
        out_specs=(ANY, VMEM),
        scratch_shapes=[
            pltpu.VMEM((blocks_col, 2, rows, BLK), jnp.bfloat16),
            pltpu.VMEM((2, NSN, 2, listed, BLK, half), jnp.bfloat16),
            pltpu.VMEM(side, jnp.float32),
            pltpu.VMEM(side, jnp.float32),
            pltpu.VMEM(side, jnp.float32),
            pltpu.VMEM((per * 2 * BLK, 4 * BLK), jnp.bfloat16),
            pltpu.VMEM((size, half), jnp.float32),
            pltpu.VMEM((n, size // n, half), jnp.float32),
            dma((blocks_col,)), dma, dma((nz + 2,)), dma((nz,)), dma((nz,)), dma((nz,)), dma((n,)), dma((n,)),
            dma((NSN,)), dma((NSN,)), dma((NSN,)), dma((n,)), dma((n,)), dma((n,)), dma((n,)),
        ],
        compiler_params=pltpu.CompilerParams(
            collective_id=0, has_side_effects=True, vmem_limit_bytes=66000000),
        name="inversion_step",
    )(pick, keep, local_pick, local_keep, shards, inverse_pairs)
    schur = diag_blocks.astype(jnp.float32) - correction.reshape(diag_blocks.shape)
    return (values, schur)


def solution(mesh):
    in_specs = (
        P("pole", "row", "col"),
        P("pole", None, "row", "col"),
        P("pole", None, None, "col"),
        P(),
        P(),
    )
    out_specs = (P("pole", None, "row", "col"), P("pole", None, None, "col"))
    return jax.shard_map(functools.partial(local, mesh.shape["row"]), mesh=mesh, in_specs=in_specs,
                         out_specs=out_specs, check_vma=False)
```

```python
import functools

import jax
import jax.numpy as jnp
from jax import lax
from jax.experimental import pallas as pl
from jax.experimental.pallas import tpu as pltpu
from jax.sharding import PartitionSpec as P

NSN = 2
BLK = 128
MESH = pl.DeviceIdType.MESH
ANY = pl.BlockSpec(memory_space=pl.ANY)
VMEM = pl.BlockSpec(memory_space=pltpu.VMEM)
SMEM = pl.BlockSpec(memory_space=pltpu.SMEM)


def aligned(start, size):
    return pl.ds(pl.multiple_of(start, size), size)


def kernel(n, ny, pick, keep, local_pick, local_keep, x_ref, a_ref, out_ref, sum_ref,
           a_buf, g_ref, own, oth, recv, bbuf, mine, parts,
           a_sem, loc_sem, z_send, z_recv, y_send, y_recv, s_send, s_recv,
           v_send, v_recv, o_sem, r_send, r_recv, b_send, b_recv):
    nz = n // ny
    span = g_ref.shape[3] * BLK // n
    rows = a_ref.shape[1]
    blocks_col = a_ref.shape[2] // BLK
    blocks_row = rows // BLK
    tile = 512 if rows % 512 == 0 else 384 if rows % 384 == 0 else BLK
    per = max(1, span // BLK)
    unit = min(span, BLK)
    row = lax.axis_index("row")
    col = lax.axis_index("col")
    z = row // ny
    y = row % ny
    oy = ny - 1 - y
    sibling = {"col": 1 - col}
    up = {"row": row + ny}
    down = {"row": row - ny}
    across = {"row": z * ny + oy}

    def stream(b):
        return pltpu.make_async_copy(a_ref.at[:, :, aligned(b * BLK, BLK)], a_buf.at[b], a_sem.at[b])

    def start_stream(b, carry):
        stream(b).start()
        return carry

    def wait_stream(b, carry):
        stream(b).wait()
        return carry

    def slot(c, r):
        if span >= BLK:
            return g_ref.at[c, :, :, pl.ds(r * per, per)]
        return g_ref.at[c, :, :, r * span // BLK, aligned(r * span % BLK, span)]

    local = pltpu.make_async_copy(x_ref, slot(col, row), loc_sem)
    local.start()

    barrier = pltpu.get_barrier_semaphore()
    pl.semaphore_signal(barrier, inc=1, device_id=sibling, device_id_type=MESH)
    for d in range(1, n):
        pl.semaphore_signal(barrier, inc=1, device_id={"row": (row + d) % n}, device_id_type=MESH)
    pl.semaphore_wait(barrier, n)

    def copy(src, c, r, send, got, target):
        return pltpu.make_async_remote_copy(
            src_ref=src, dst_ref=slot(c, r), send_sem=send, recv_sem=got,
            device_id=target, device_id_type=MESH)

    def line(src, zz, target):
        return copy(src, col, zz * ny + y, z_send.at[zz], z_recv.at[zz], target)

    def side(src, zz, yy):
        return copy(src, col, zz * ny + yy, y_send.at[zz], y_recv.at[zz], across)

    def sib(src, c, r):
        return copy(src, c, r, s_send.at[r], s_recv.at[r], sibling)

    def here(zz, yy):
        return slot(col, zz * ny + yy)

    first_up = copy(x_ref, col, row, z_send.at[nz], z_recv.at[z], up)
    first_down = copy(x_ref, col, row, z_send.at[nz + 1], z_recv.at[z], down)
    pl.when(z < nz - 1)(lambda: first_up.start())
    pl.when(z > 0)(lambda: first_down.start())
    side(x_ref, z, y).start()
    sib(x_ref, col, row).start()
    lax.fori_loop(0, blocks_col, start_stream, 0)
    own[...] = jnp.zeros_like(own)
    oth[...] = jnp.zeros_like(oth)
    mine[...] = jnp.zeros_like(mine)
    local.wait()

    def from_line(zz, forward, target):
        line(here(zz, y), zz, target).wait_recv()

        @pl.when(forward)
        def _():
            line(here(zz, y), zz, target).start()

        side(here(zz, y), zz, y).start()
        sib(here(zz, y), col, zz * ny + y).start()

    def from_side(zz):
        side(here(zz, oy), zz, oy).wait_recv()
        sib(here(zz, oy), col, zz * ny + oy).start()

    outs = (own, oth)

    def multiply(r):
        sib(slot(1 - col, r), 1 - col, r).wait_recv()

        def supernode(k, carry):
            if unit < BLK:
                bbuf[...] = jnp.zeros_like(bbuf)
            for e in range(per):
                start = r * span + e * BLK
                scale = keep[k, start // BLK]
                base = e * 2 * BLK
                if unit < BLK:
                    shift = start % BLK
                    top = aligned(base + shift, unit)
                    low = aligned(base + BLK + shift, unit)
                else:
                    top = pl.ds(base, unit)
                    low = pl.ds(base + BLK, unit)
                for rel in range(2):
                    c = col if rel == 0 else 1 - col
                    at = pl.ds(0, unit) if unit == BLK else aligned(start % BLK, unit)
                    real = (g_ref[c, k, 0, start // BLK, at, :].astype(jnp.float32) * scale).astype(jnp.bfloat16)
                    imag = (g_ref[c, k, 1, start // BLK, at, :].astype(jnp.float32) * scale).astype(jnp.bfloat16)
                    left = rel * 2 * BLK
                    bbuf[top, left:left + BLK] = -real
                    bbuf[top, left + BLK:left + 2 * BLK] = -imag
                    bbuf[low, left:left + BLK] = imag
                    bbuf[low, left + BLK:left + 2 * BLK] = -real

            def by_tile(t, inner):
                at = aligned(t * tile, tile)
                pieces = []
                for e in range(per):
                    block = pick[k, (r * span + e * BLK) // BLK]
                    pieces += [a_buf[block, 0, at, :], a_buf[block, 1, at, :]]
                left = jnp.concatenate(pieces, axis=1)
                for rel in range(2):
                    found = jnp.dot(left, bbuf[:, rel * 2 * BLK:(rel + 1) * 2 * BLK],
                                    preferred_element_type=jnp.float32)
                    outs[rel][k, 0, at, :] += found[:, :BLK]
                    outs[rel][k, 1, at, :] += found[:, BLK:]
                return inner

            lax.fori_loop(0, rows // tile, by_tile, 0)
            return carry

        lax.fori_loop(0, NSN, supernode, 0)

    def one_round(d, carry):
        pl.when(z - d >= 0)(lambda: from_line(z - d, z < nz - 1, up))
        pl.when(z + d < nz)(lambda: from_line(z + d, z > 0, down))
        pl.when(z - d + 1 >= 0)(lambda: from_side(z - d + 1))
        pl.when((d > 1) & (z + d - 1 < nz))(lambda: from_side(z + d - 1))

        @pl.when(d == 2)
        def _():
            lax.fori_loop(0, blocks_col, wait_stream, 0)


        def late(q, inner):
            away = d - 2 - q // 2
            zz = z + jnp.where(q % 2 == 0, -away, away)
            yy = jnp.where(q // 2 == 0, y, oy)
            valid = (away >= 0) & (zz >= 0) & (zz < nz) & ((away > 0) | (q % 2 == 0))
            pl.when(valid)(lambda: multiply(zz * ny + yy))
            return inner

        lax.fori_loop(0, 4, late, 0)
        return carry

    lax.fori_loop(1, nz + 3, one_round, 0)

    def swap(k):
        return pltpu.make_async_remote_copy(
            src_ref=oth.at[k], dst_ref=recv.at[k], send_sem=v_send.at[k], recv_sem=v_recv.at[k],
            device_id=sibling, device_id_type=MESH)

    for k in range(NSN):
        swap(k).start()
    for r in range(n):
        sib(slot(col, r), col, r).wait_send()
    for zz in range(nz):
        side(here(zz, y), zz, y).wait_send()
        pl.when(((zz < z) & (z < nz - 1)) | ((zz > z) & (z > 0)))(
            lambda: line(here(zz, y), zz, up).wait_send())
    pl.when(z < nz - 1)(lambda: first_up.wait_send())
    pl.when(z > 0)(lambda: first_down.wait_send())

    size = sum_ref.shape[0] // (NSN * n)

    def place(k, r):
        return aligned(k * n * size + r * size, size)

    def scatter(k, d):
        to = (row + d) % n
        return pltpu.make_async_remote_copy(
            src_ref=mine.at[place(k, to)], dst_ref=parts.at[k, d],
            send_sem=r_send.at[k, d], recv_sem=r_recv.at[k, d],
            device_id={"row": to}, device_id_type=MESH)

    def spread(k, d):
        return pltpu.make_async_remote_copy(
            src_ref=parts.at[k, 0], dst_ref=sum_ref.at[place(k, row)],
            send_sem=b_send.at[k, d], recv_sem=b_recv.at[k, d],
            device_id={"row": (row + d) % n}, device_id_type=MESH)

    group = 3 if blocks_row % 3 == 0 else 1
    width = 2 * BLK
    for k in range(NSN):
        swap(k).wait_recv()
        own[k] += recv[k]
        pltpu.make_async_copy(own.at[k], out_ref.at[k], o_sem.at[k]).start()

        def correct(s, carry, k=k):
            left, right = [], []
            for u in range(group):
                t = s * group + u
                j = local_pick[k, t]
                scale = local_keep[k, t]
                for p in range(2):
                    left.append(jnp.concatenate([g_ref[0, k, p, j], g_ref[1, k, p, j]], axis=1))
                real = own[k, 0, aligned(t * BLK, BLK), :] * scale
                imag = own[k, 1, aligned(t * BLK, BLK), :] * scale
                right.append(jnp.concatenate([real, imag], axis=1))
                right.append(jnp.concatenate([-imag, real], axis=1))
            factor = jnp.concatenate(left, axis=0)
            wide = jnp.concatenate(right, axis=0)
            total = None
            for _ in range(2):
                piece = wide.astype(jnp.bfloat16)
                wide = wide - piece.astype(jnp.float32)
                term = lax.dot_general(factor, piece, (((0,), (0,)), ((), ())),
                                       preferred_element_type=jnp.float32)
                total = term if total is None else total + term
            mine[2 * k * width:(2 * k + 1) * width, :] += total[:, :BLK]
            mine[(2 * k + 1) * width:(2 * k + 2) * width, :] += total[:, BLK:]
            return carry

        lax.fori_loop(0, blocks_row // group, correct, 0)
        for d in range(1, n):
            scatter(k, d).start()


    for k in range(NSN):
        total = mine[place(k, row), :]
        for d in range(1, n):
            scatter(k, d).wait_recv()
            total = total + parts[k, d]
        parts[k, 0] = total
        sum_ref[place(k, row), :] = total
        for d in range(1, n):
            spread(k, d).start()
    for k in range(NSN):
        swap(k).wait_send()
        pltpu.make_async_copy(own.at[k], out_ref.at[k], o_sem.at[k]).wait()
        for d in range(1, n):
            scatter(k, d).wait_send()
            spread(k, d).wait()


def local(n, inverse_pairs, factor_rows, diag_blocks, row_lists, block_order):
    rows, cols = inverse_pairs.shape[1:]
    blocks_row, blocks_col = rows // BLK, cols // BLK
    listed = row_lists.shape[1]
    hits = row_lists[:, :, None] == block_order[None, None, :]
    storage = jnp.arange(block_order.shape[0], dtype=jnp.int32)
    position = jnp.sum(jnp.where(hits, storage, 0), axis=2).astype(jnp.int32)
    pick = position - lax.axis_index("col") * blocks_col
    keep = ((pick >= 0) & (pick < blocks_col)).astype(jnp.float32)
    pick = jnp.clip(pick, 0, blocks_col - 1)
    place = lax.axis_index("row") * blocks_row + jnp.arange(blocks_row, dtype=jnp.int32)
    found = position[:, None, :] == place[None, :, None]
    local_pick = jnp.sum(jnp.where(found, jnp.arange(listed, dtype=jnp.int32), 0), axis=2).astype(jnp.int32)
    local_keep = jnp.sum(found.astype(jnp.float32), axis=2)

    ny = 2 if n % 2 == 0 else 1
    nz = n // ny
    span, half = factor_rows.shape[2:]
    size = NSN * 2 * 2 * half
    per = max(1, span // BLK)
    shards = factor_rows.reshape(NSN, 2, per, BLK, half) if span >= BLK else factor_rows
    dma = pltpu.SemaphoreType.DMA
    side = (NSN, 2, rows, half)
    values, correction = pl.pallas_call(
        functools.partial(kernel, n, ny),
        out_shape=(jax.ShapeDtypeStruct(side, jnp.float32), jax.ShapeDtypeStruct((size, half), jnp.float32)),
        in_specs=[SMEM, SMEM, SMEM, SMEM, ANY, ANY],
        out_specs=(ANY, VMEM),
        scratch_shapes=[
            pltpu.VMEM((blocks_col, 2, rows, BLK), jnp.bfloat16),
            pltpu.VMEM((2, NSN, 2, listed, BLK, half), jnp.bfloat16),
            pltpu.VMEM(side, jnp.float32),
            pltpu.VMEM(side, jnp.float32),
            pltpu.VMEM(side, jnp.float32),
            pltpu.VMEM((per * 2 * BLK, 4 * BLK), jnp.bfloat16),
            pltpu.VMEM((size, half), jnp.float32),
            pltpu.VMEM((NSN, n, size // (NSN * n), half), jnp.float32),
            dma((blocks_col,)), dma, dma((nz + 2,)), dma((nz,)), dma((nz,)), dma((nz,)), dma((n,)), dma((n,)),
            dma((NSN,)), dma((NSN,)), dma((NSN,)), dma((NSN, n)), dma((NSN, n)), dma((NSN, n)), dma((NSN, n)),
        ],
        compiler_params=pltpu.CompilerParams(
            collective_id=0, has_side_effects=True, vmem_limit_bytes=66000000),
        name="inversion_step",
    )(pick, keep, local_pick, local_keep, shards, inverse_pairs)
    schur = diag_blocks.astype(jnp.float32) - correction.reshape(diag_blocks.shape)
    return (values, schur)


def solution(mesh):
    in_specs = (
        P("pole", "row", "col"),
        P("pole", None, "row", "col"),
        P("pole", None, None, "col"),
        P(),
        P(),
    )
    out_specs = (P("pole", None, "row", "col"), P("pole", None, None, "col"))
    return jax.shard_map(functools.partial(local, mesh.shape["row"]), mesh=mesh, in_specs=in_specs,
                         out_specs=out_specs, check_vma=False)
```
